32 devices in a mesh: rows: 8 (over z, y), mp: 4 (over x, core).
Axes of the slice: x: 2, y: 2, z: 4, core: 2. Of those that a mesh axis runs over, the one named last changes fastest.
Arguments:
- calib: bfloat16 [512, 8192], P('rows', 'mp'), may hold values from -40 to 40
- weight: bfloat16 [8192, 8192], P('rows', 'mp'), may hold values from -6 to 6
- inverse_factor: float32 [8192, 8192], P('rows', 'mp'), may hold values from -10 to 12, as said below
- pruned_blocks: int32 [7], replicated, may hold values from 0 to 63, as said below
Outputs:
- pruned_weight: bfloat16 [8192, 8192], P('rows', 'mp')
- next_gram: float32 [8192, 8192], P('rows', 'mp')
The draws below stay inside these ranges and needn't reach their ends.
Inputs may be any that keep to these rules, and one draw needn't show every extreme that they name: `pruned_blocks`: 7 distinct block numbers in any order; block b holds rows b * 128 to b * 128 + 127. `inverse_factor`: symmetric and positive definite.
All inputs are finite; a program needn't handle non-finite values.
Results may differ from the reference program's by a relative error of at most 0.0095.
Values may be sent and summed in bfloat16 or wider, within the bound.
A program may use at most 128 MiB of HBM per device.

```python
import jax
import jax.numpy as jnp
from jax import lax

D = 8192
BLOCK = 128
NB = 7
TOKENS = 512


def draw_calib(key, part):
    first, second, third = jax.random.split(jax.random.fold_in(key, 31), 3)
    row_scale = jnp.exp(jax.random.uniform(first, (TOKENS, 1), jnp.float32, jnp.log(0.3), jnp.log(3.0)))
    col_scale = jnp.exp(jax.random.uniform(second, (1, D), jnp.float32, jnp.log(0.5), jnp.log(2.0)))
    values = jax.random.normal(third, (TOKENS, D), jnp.float32)
    return jnp.clip(values * row_scale * col_scale, -40.0, 40.0).astype(jnp.bfloat16)


def draw_inverse_factor(key, part):
    first, second, third = jax.random.split(jax.random.fold_in(key, 11), 3)
    factor_rank = max(NB * BLOCK // 4, 4)
    coeff = 0.003 / jnp.sqrt(2.0 * D)
    noise = jax.random.normal(first, (D, D), jnp.float32)
    diagonal = jnp.exp(jax.random.uniform(second, (D,), jnp.float32, jnp.log(0.02), jnp.log(2.0)))
    loadings = jnp.clip(jax.random.normal(third, (D, factor_rank), jnp.float32), -3.0, 3.0)
    noise = jnp.clip(noise, -6.0, 6.0)
    shared = jnp.dot(loadings, loadings.T, precision=lax.Precision.HIGHEST) * (1.0 / factor_rank)
    shared = 0.5 * (shared + shared.T)
    return (noise + noise.T) * coeff + shared + jnp.diag(diagonal)


def draw_pruned_blocks(key, part):
    first, second = jax.random.split(jax.random.fold_in(key, 5), 2)
    inner = jax.random.permutation(first, D // BLOCK - 2)[:NB - 2].astype(jnp.int32) + 1
    ends = jnp.array([0, D // BLOCK - 1], dtype=jnp.int32)
    blocks = jnp.concatenate([ends, inner])
    order = jax.random.permutation(second, NB)
    return blocks[order].astype(jnp.int32)


def levels(key, extent, shards, smallest, high):
    def one(axis_at, parts):
        draws = jax.random.uniform(jax.random.fold_in(jax.random.fold_in(key, 6), axis_at), (parts,), jnp.float32, smallest / len(shards), high / len(shards))
        return jnp.repeat(jnp.exp(draws), extent[axis_at] // parts).reshape((-1,) + (1,) * (len(extent) - axis_at - 1))

    level = one(*shards[0])
    for cut in shards[1:]:
        level = level * one(*cut)
    return level


def scatter_about(own_key, extent, width, reach, cuts=(), kind=jnp.bfloat16):
    values = jax.random.normal(own_key, extent, jnp.float32) * width
    if len(cuts) > 0:
        values = levels(own_key, extent, cuts, -0.22, 0.18) * values
    return jnp.clip(values, min=-reach, max=reach).astype(kind)


def setup_inputs(seed: int = 0) -> dict:
    streams_of = jax.random.split(jax.random.key(seed), 5)
    return {
        "calib": draw_calib(jax.random.fold_in(streams_of[4], 71), 0),
        "weight": scatter_about(streams_of[1], (D, D), 1.0, 6.0, ((0, 8), (1, 4))),
        "inverse_factor": draw_inverse_factor(jax.random.fold_in(streams_of[4], 71), 0),
        "pruned_blocks": draw_pruned_blocks(jax.random.fold_in(streams_of[4], 71), 0),
    }


def spd_solve(chol_lower, right_side):
    forward = lax.linalg.triangular_solve(chol_lower, right_side, left_side=True, lower=True)
    return lax.linalg.triangular_solve(chol_lower, forward, left_side=True, lower=True, transpose_a=True)

def reference(calib, weight, inverse_factor, pruned_blocks):
    row_numbers = (pruned_blocks[:, None] * BLOCK + jnp.arange(BLOCK, dtype=jnp.int32)[None, :]).reshape(-1).astype(jnp.int32)
    columns = jnp.take(inverse_factor, row_numbers, axis=1)
    square = jnp.take(columns, row_numbers, axis=0)
    kept_rows = jnp.take(weight, row_numbers, axis=0).astype(jnp.float32)
    chol_lower = jnp.linalg.cholesky(square)
    solved = spd_solve(chol_lower, kept_rows)
    update = jnp.dot(columns, solved, precision=lax.Precision.HIGHEST)
    block_ids = jnp.arange(D, dtype=jnp.int32) // BLOCK
    kept_mask = 1.0 - jnp.any(block_ids[:, None] == pruned_blocks[None, :], axis=1).astype(jnp.float32)
    pruned_weight = ((weight.astype(jnp.float32) - update) * kept_mask[:, None]).astype(jnp.bfloat16)
    projected = jnp.dot(calib.astype(jnp.float32), pruned_weight.T.astype(jnp.float32), preferred_element_type=jnp.float32)
    outputs = (projected * float(D) ** (-0.5)).astype(jnp.bfloat16)
    next_gram = jnp.dot(outputs.T.astype(jnp.float32), outputs.astype(jnp.float32), preferred_element_type=jnp.float32) / TOKENS
    return (pruned_weight, next_gram)
```

```python
import jax
import jax.numpy as jnp
from jax import lax
from jax.experimental import pallas as pl
from jax.experimental.pallas import tpu as pltpu
from jax.sharding import PartitionSpec as P

BLOCK = 128
SUB = 8


def split3(value):
    first = value.astype(jnp.bfloat16)
    rest = value - first.astype(jnp.float32)
    second = rest.astype(jnp.bfloat16)
    third = (rest - second.astype(jnp.float32)).astype(jnp.bfloat16)
    return first, second, third


def sweep_block(tiles):
    lane = lax.broadcasted_iota(jnp.int32, (SUB, BLOCK), 1)
    sublane = lax.broadcasted_iota(jnp.int32, (SUB, BLOCK), 0)
    wide = (SUB, BLOCK)
    for p in range(0, BLOCK, 2):
        q = p + 1
        own, s = p // SUB, p % SUB
        row_p = jnp.broadcast_to(tiles[own][s : s + 1, :], wide)
        row_q = jnp.broadcast_to(tiles[own][s + 1 : s + 2, :], wide)
        d_p = jnp.broadcast_to(row_p[:, p : p + 1], wide)
        off = jnp.broadcast_to(row_p[:, q : q + 1], wide)
        d_q = jnp.broadcast_to(row_q[:, q : q + 1], wide)
        inv_p = 1.0 / d_p
        ratio = off * inv_p
        m_qq = 1.0 / (d_q - off * ratio)
        m_pq = -ratio * m_qq
        m_pp = inv_p - ratio * m_pq
        is_p, is_q = lane == p, lane == q
        u_p = m_pp * row_p + m_pq * row_q
        u_q = m_pq * row_p + m_qq * row_q
        u_p = jnp.where(is_p, -m_pp, jnp.where(is_q, -m_pq, u_p))
        u_q = jnp.where(is_p, -m_pq, jnp.where(is_q, -m_qq, u_q))
        pivot = is_p | is_q
        new = []
        for t in range(len(tiles)):
            col_p = jnp.broadcast_to(tiles[t][:, p : p + 1], wide)
            col_q = jnp.broadcast_to(tiles[t][:, q : q + 1], wide)
            value = jnp.where(pivot, 0.0, tiles[t]) - col_p * u_p - col_q * u_q
            if t == own:
                value = jnp.where(sublane == s, u_p, jnp.where(sublane == s + 1, u_q, value))
            new.append(value)
        tiles = new
    return tiles


def invert_kernel(low_ref, out_ref, neg_ref, rhs_ref, pivot_ref):
    count = out_ref.shape[0] // BLOCK
    at = 0
    for i in range(count):
        for j in range(i + 1):
            block = low_ref[:, at : at + BLOCK]
            at += BLOCK
            out_ref[i * BLOCK : (i + 1) * BLOCK, j * BLOCK : (j + 1) * BLOCK] = block
            if j < i:
                out_ref[j * BLOCK : (j + 1) * BLOCK, i * BLOCK : (i + 1) * BLOCK] = block.T

    def stage(k, carry):
        here = pl.ds(pl.multiple_of(k * BLOCK, BLOCK), BLOCK)
        diag = out_ref[here, here]
        tiles = [diag[t * SUB : (t + 1) * SUB, :] for t in range(BLOCK // SUB)]
        tiles = sweep_block(tiles)
        for t in range(BLOCK // SUB):
            neg_ref[t * SUB : (t + 1) * SUB, :] = tiles[t]
        neg = neg_ref[...]
        r1, r2, r3 = split3(out_ref[here, :])
        a1, a2, a3 = split3(-neg)
        pivot_ref[...] = jnp.dot(
            jnp.concatenate([a1, a1, a2, a2, a1, a3], axis=1),
            jnp.concatenate([r1, r2, r1, r2, r3, r1], axis=0),
            preferred_element_type=jnp.float32,
        )
        pivot_ref[:, here] = neg
        b1, b2, b3 = split3(pivot_ref[...])
        for slot, part in enumerate((b1, b2, b1, b2, b3, b1)):
            rhs_ref[slot * BLOCK : (slot + 1) * BLOCK, :] = part

        def update(i, inner):
            rows = pl.ds(pl.multiple_of(i * BLOCK, BLOCK), BLOCK)
            c1, c2, c3 = split3(out_ref[rows, here])
            out_ref[rows, here] = jnp.zeros((BLOCK, BLOCK), jnp.float32)
            out_ref[rows, :] -= jnp.dot(
                jnp.concatenate([c1, c1, c2, c2, c1, c3], axis=1),
                rhs_ref[...],
                preferred_element_type=jnp.float32,
            )
            return inner

        lax.fori_loop(0, count, update, 0)
        out_ref[here, :] = pivot_ref[...]
        return carry

    lax.fori_loop(0, count, stage, 0)


def minus_inverse(low, order):
    vmem = pl.BlockSpec(memory_space=pltpu.VMEM)
    return pl.pallas_call(
        invert_kernel,
        out_shape=jax.ShapeDtypeStruct((order, order), jnp.float32),
        in_specs=[vmem],
        out_specs=vmem,
        scratch_shapes=[
            pltpu.VMEM((BLOCK, BLOCK), jnp.float32),
            pltpu.VMEM((6 * BLOCK, order), jnp.bfloat16),
            pltpu.VMEM((BLOCK, order), jnp.float32),
        ],
        compiler_params=pltpu.CompilerParams(vmem_limit_bytes=32 * 1024 * 1024),
        cost_estimate=pl.CostEstimate(
            flops=60_000_000_000, bytes_accessed=2 * order * order * 4, transcendentals=0
        ),
    )(low)


def shards(calib, weight, inverse_factor, pruned_blocks):
    rows_dev = weight.shape[0]
    width_dev = weight.shape[1]
    row_parts = lax.axis_size("rows")
    mp_parts = lax.axis_size("mp")
    full_width = width_dev * mp_parts
    row_start = lax.axis_index("rows") * rows_dev
    col_start = lax.axis_index("mp") * width_dev
    starts = pruned_blocks * BLOCK
    block_count = pruned_blocks.shape[0]
    col_pieces = []
    for slot_index in range(block_count):
        offset = starts[slot_index] - col_start
        inside = (offset >= 0) & (offset < width_dev)
        clamped = jnp.clip(offset, 0, width_dev - BLOCK)
        piece = lax.dynamic_slice_in_dim(inverse_factor, clamped, BLOCK, 1)
        col_pieces.append(jnp.where(inside, piece, 0.0))
    columns = jnp.concatenate(col_pieces, axis=1)
    weight_parts = []
    low_parts = []
    for slot_index in range(block_count):
        offset = starts[slot_index] - row_start
        inside = (offset >= 0) & (offset < rows_dev)
        clamped = jnp.clip(offset, 0, rows_dev - BLOCK)
        piece = lax.dynamic_slice_in_dim(weight, clamped, BLOCK, 0)
        weight_parts.append(jnp.where(inside, piece, jnp.zeros_like(piece)))
        piece = lax.dynamic_slice(columns, (clamped, 0), (BLOCK, (slot_index + 1) * BLOCK))
        low_parts.append(jnp.where(inside, piece, 0.0))
    low = lax.psum(jnp.concatenate(low_parts, axis=1), ("rows", "mp"))
    own_columns = lax.psum_scatter(columns, "mp", scatter_dimension=0, tiled=True)
    kept_rows = lax.psum(jnp.concatenate(weight_parts, axis=0), "rows")
    all_calib = lax.all_gather(calib, "rows", axis=0, tiled=True)

    negative = minus_inverse(low, block_count * BLOCK)
    own_factors = -lax.dot_general(
        own_columns,
        negative,
        (((1,), (0,)), ((), ())),
        precision=lax.Precision.HIGHEST,
        preferred_element_type=jnp.float32,
    )
    factors = lax.all_gather(own_factors.astype(jnp.bfloat16), "mp", axis=0, tiled=True)
    update = lax.dot_general(
        factors, kept_rows, (((1,), (0,)), ((), ())), preferred_element_type=jnp.float32
    )
    block_ids = (row_start + jnp.arange(rows_dev, dtype=jnp.int32)) // BLOCK
    pruned = jnp.any(block_ids[:, None] == pruned_blocks[None, :], axis=1)
    pruned_weight = jnp.where(
        pruned[:, None], 0.0, weight.astype(jnp.float32) - update
    ).astype(jnp.bfloat16)
    out_scale = float(full_width) ** (-0.5)
    partial_value = lax.dot_general(
        all_calib, pruned_weight, (((1,), (1,)), ((), ())), preferred_element_type=jnp.float32
    )
    token_count = partial_value.shape[0]
    own_rows = lax.psum_scatter(
        (partial_value * out_scale).astype(jnp.bfloat16), "mp", scatter_dimension=0, tiled=True
    )
    per_col = row_parts // mp_parts
    pairs = []
    for r in range(row_parts):
        for m in range(mp_parts):
            target = ((r % per_col) * mp_parts + m) * mp_parts + r // per_col
            pairs.append((r * mp_parts + m, target))
    moved = lax.ppermute(own_rows, ("rows", "mp"), pairs)
    left = lax.all_gather(own_rows, "mp", axis=0, tiled=True)
    right = lax.all_gather(moved, "rows", axis=0, tiled=False)
    right = right.reshape(per_col, token_count, rows_dev)
    gram_pieces = [
        lax.dot_general(
            left, right[c], (((0,), (0,)), ((), ())), preferred_element_type=jnp.float32
        )
        for c in range(per_col)
    ]
    gram_block = jnp.concatenate(gram_pieces, axis=1) / token_count
    return (pruned_weight, gram_block)


def solution(mesh):
    return jax.shard_map(
        shards,
        mesh=mesh,
        in_specs=(P("rows", "mp"), P("rows", "mp"), P("rows", "mp"), P()),
        out_specs=(P("rows", "mp"), P("rows", "mp")),
        check_vma=False,
    )
```

```python
import functools

import jax
import jax.numpy as jnp
from jax import lax
from jax.experimental import pallas as pl
from jax.experimental.pallas import tpu as pltpu
from jax.sharding import PartitionSpec as P

BLOCK = 128
SUB = 8


def split3(value):
    first = value.astype(jnp.bfloat16)
    rest = value - first.astype(jnp.float32)
    second = rest.astype(jnp.bfloat16)
    third = (rest - second.astype(jnp.float32)).astype(jnp.bfloat16)
    return first, second, third


def sweep_block(tiles):
    lane = lax.broadcasted_iota(jnp.int32, (SUB, BLOCK), 1)
    sublane = lax.broadcasted_iota(jnp.int32, (SUB, BLOCK), 0)
    wide = (SUB, BLOCK)
    for p in range(0, BLOCK, 2):
        q = p + 1
        own, s = p // SUB, p % SUB
        row_p = jnp.broadcast_to(tiles[own][s : s + 1, :], wide)
        row_q = jnp.broadcast_to(tiles[own][s + 1 : s + 2, :], wide)
        d_p = jnp.broadcast_to(row_p[:, p : p + 1], wide)
        off = jnp.broadcast_to(row_p[:, q : q + 1], wide)
        d_q = jnp.broadcast_to(row_q[:, q : q + 1], wide)
        inv_p = 1.0 / d_p
        ratio = off * inv_p
        m_qq = 1.0 / (d_q - off * ratio)
        m_pq = -ratio * m_qq
        m_pp = inv_p - ratio * m_pq
        is_p, is_q = lane == p, lane == q
        u_p = m_pp * row_p + m_pq * row_q
        u_q = m_pq * row_p + m_qq * row_q
        u_p = jnp.where(is_p, -m_pp, jnp.where(is_q, -m_pq, u_p))
        u_q = jnp.where(is_p, -m_pq, jnp.where(is_q, -m_qq, u_q))
        pivot = is_p | is_q
        new = []
        for t in range(len(tiles)):
            col_p = jnp.broadcast_to(tiles[t][:, p : p + 1], wide)
            col_q = jnp.broadcast_to(tiles[t][:, q : q + 1], wide)
            value = jnp.where(pivot, 0.0, tiles[t]) - col_p * u_p - col_q * u_q
            if t == own:
                value = jnp.where(sublane == s, u_p, jnp.where(sublane == s + 1, u_q, value))
            new.append(value)
        tiles = new
    return tiles


def invert_kernel(low_ref, out_ref, neg_ref, rhs_ref, pivot_ref):
    count = out_ref.shape[0] // BLOCK
    at = 0
    for i in range(count):
        for j in range(i + 1):
            block = low_ref[:, at : at + BLOCK]
            at += BLOCK
            out_ref[i * BLOCK : (i + 1) * BLOCK, j * BLOCK : (j + 1) * BLOCK] = block
            if j < i:
                out_ref[j * BLOCK : (j + 1) * BLOCK, i * BLOCK : (i + 1) * BLOCK] = block.T

    def stage(k, carry):
        here = pl.ds(pl.multiple_of(k * BLOCK, BLOCK), BLOCK)
        diag = out_ref[here, here]
        tiles = [diag[t * SUB : (t + 1) * SUB, :] for t in range(BLOCK // SUB)]
        tiles = sweep_block(tiles)
        for t in range(BLOCK // SUB):
            neg_ref[t * SUB : (t + 1) * SUB, :] = tiles[t]
        neg = neg_ref[...]
        r1, r2, r3 = split3(out_ref[here, :])
        a1, a2, a3 = split3(-neg)
        pivot_ref[...] = jnp.dot(
            jnp.concatenate([a1, a1, a2, a2, a1, a3], axis=1),
            jnp.concatenate([r1, r2, r1, r2, r3, r1], axis=0),
            preferred_element_type=jnp.float32,
        )
        pivot_ref[:, here] = neg
        b1, b2, b3 = split3(pivot_ref[...])
        for slot, part in enumerate((b1, b2, b1, b2, b3, b1)):
            rhs_ref[slot * BLOCK : (slot + 1) * BLOCK, :] = part

        def update(i, inner):
            rows = pl.ds(pl.multiple_of(i * BLOCK, BLOCK), BLOCK)
            c1, c2, c3 = split3(out_ref[rows, here])
            out_ref[rows, here] = jnp.zeros((BLOCK, BLOCK), jnp.float32)
            out_ref[rows, :] -= jnp.dot(
                jnp.concatenate([c1, c1, c2, c2, c1, c3], axis=1),
                rhs_ref[...],
                preferred_element_type=jnp.float32,
            )
            return inner

        lax.fori_loop(0, count, update, 0)
        out_ref[here, :] = pivot_ref[...]
        return carry

    lax.fori_loop(0, count, stage, 0)


def minus_inverse(low, order):
    vmem = pl.BlockSpec(memory_space=pltpu.VMEM)
    return pl.pallas_call(
        invert_kernel,
        out_shape=jax.ShapeDtypeStruct((order, order), jnp.float32),
        in_specs=[vmem],
        out_specs=vmem,
        scratch_shapes=[
            pltpu.VMEM((BLOCK, BLOCK), jnp.float32),
            pltpu.VMEM((6 * BLOCK, order), jnp.bfloat16),
            pltpu.VMEM((BLOCK, order), jnp.float32),
        ],
        compiler_params=pltpu.CompilerParams(vmem_limit_bytes=32 * 1024 * 1024),
        cost_estimate=pl.CostEstimate(
            flops=60_000_000_000, bytes_accessed=2 * order * order * 4, transcendentals=0
        ),
    )(low)


def pick_columns_kernel(places_ref, factor_ref, columns_ref, low_ref):
    j = pl.program_id(0)
    columns_ref[...] = jnp.where(places_ref[1, j] != 0, factor_ref[...], 0.0)
    for i in range(places_ref.shape[1]):

        @pl.when(i >= j)
        def _():
            rows = pl.ds(pl.multiple_of(places_ref[2, i] * BLOCK, BLOCK), BLOCK)
            lanes = pl.ds(pl.multiple_of((i * (i + 1) // 2 + j) * BLOCK, BLOCK), BLOCK)
            low_ref[:, lanes] = jnp.where(places_ref[3, i] != 0, columns_ref[rows, :], 0.0)


def pick_columns(places, factor):
    count = places.shape[1]
    rows = factor.shape[0]
    lanes = count * (count + 1) // 2 * BLOCK
    return pl.pallas_call(
        pick_columns_kernel,
        out_shape=(
            jax.ShapeDtypeStruct((rows, count * BLOCK), jnp.float32),
            jax.ShapeDtypeStruct((BLOCK, lanes), jnp.float32),
        ),
        grid_spec=pltpu.PrefetchScalarGridSpec(
            num_scalar_prefetch=1,
            grid=(count,),
            in_specs=[pl.BlockSpec((rows, BLOCK), lambda j, places: (0, places[0, j]))],
            out_specs=(
                pl.BlockSpec((rows, BLOCK), lambda j, places: (0, j)),
                pl.BlockSpec((BLOCK, lanes), lambda j, places: (0, 0)),
            ),
        ),
    )(places, factor)


def pick_rows_kernel(places_ref, weight_ref, out_ref):
    inside = places_ref[3, pl.program_id(0)] != 0
    value = weight_ref[...].astype(jnp.float32)
    out_ref[...] = jnp.where(inside, value, 0.0).astype(jnp.bfloat16)


def pick_rows(places, weight):
    count = places.shape[1]
    width = weight.shape[1]
    return pl.pallas_call(
        pick_rows_kernel,
        out_shape=jax.ShapeDtypeStruct((count * BLOCK, width), jnp.bfloat16),
        grid_spec=pltpu.PrefetchScalarGridSpec(
            num_scalar_prefetch=1,
            grid=(count,),
            in_specs=[pl.BlockSpec((BLOCK, width), lambda i, places: (places[2, i], 0))],
            out_specs=pl.BlockSpec((BLOCK, width), lambda i, places: (i, 0)),
        ),
    )(places, weight)


def gram_kernel(token_count, left_ref, right_ref, out_ref):
    out_ref[...] = lax.dot_general(
        left_ref[...],
        right_ref[0],
        (((0,), (0,)), ((), ())),
        preferred_element_type=jnp.float32,
    ) / token_count


def gram_of(left, right, token_count):
    tokens, rows = left.shape
    parts, _, width = right.shape
    tile = min(rows, 256)
    return pl.pallas_call(
        functools.partial(gram_kernel, token_count),
        grid=(parts, rows // tile),
        in_specs=[
            pl.BlockSpec((tokens, tile), lambda c, i: (0, i)),
            pl.BlockSpec((1, tokens, width), lambda c, i: (c, 0, 0)),
        ],
        out_specs=pl.BlockSpec((tile, width), lambda c, i: (i, c)),
        out_shape=jax.ShapeDtypeStruct((rows, parts * width), jnp.float32),
    )(left, right)


def shards(calib, weight, inverse_factor, pruned_blocks):
    rows_dev = weight.shape[0]
    width_dev = weight.shape[1]
    row_parts = lax.axis_size("rows")
    mp_parts = lax.axis_size("mp")
    full_width = width_dev * mp_parts
    row_start = lax.axis_index("rows") * rows_dev
    col_start = lax.axis_index("mp") * width_dev
    starts = pruned_blocks * BLOCK
    block_count = pruned_blocks.shape[0]
    col_offsets = starts - col_start
    row_offsets = starts - row_start
    places = jnp.stack(
        [
            jnp.clip(col_offsets, 0, width_dev - BLOCK) // BLOCK,
            ((col_offsets >= 0) & (col_offsets < width_dev)).astype(jnp.int32),
            jnp.clip(row_offsets, 0, rows_dev - BLOCK) // BLOCK,
            ((row_offsets >= 0) & (row_offsets < rows_dev)).astype(jnp.int32),
        ]
    ).astype(jnp.int32)
    columns, own_low = pick_columns(places, inverse_factor)
    low = lax.psum(own_low, ("rows", "mp"))
    own_columns = lax.psum_scatter(columns, "mp", scatter_dimension=0, tiled=True)
    own_kept = pick_rows(places, weight)
    low, own_kept, calib = lax.optimization_barrier((low, own_kept, calib))
    kept_rows = lax.psum(own_kept, "rows")
    all_calib = lax.all_gather(calib, "rows", axis=0, tiled=True)

    negative = minus_inverse(low, block_count * BLOCK)
    negative, all_calib, own_columns = lax.optimization_barrier((negative, all_calib, own_columns))
    own_factors = -lax.dot_general(
        own_columns,
        negative,
        (((1,), (0,)), ((), ())),
        precision=lax.Precision.HIGHEST,
        preferred_element_type=jnp.float32,
    )
    factors = lax.all_gather(own_factors.astype(jnp.bfloat16), "mp", axis=0, tiled=True)
    update = lax.dot_general(
        factors, kept_rows, (((1,), (0,)), ((), ())), preferred_element_type=jnp.float32
    )
    block_ids = (row_start + jnp.arange(rows_dev, dtype=jnp.int32)) // BLOCK
    pruned = jnp.any(block_ids[:, None] == pruned_blocks[None, :], axis=1)
    pruned_weight = jnp.where(
        pruned[:, None], 0.0, weight.astype(jnp.float32) - update
    ).astype(jnp.bfloat16)
    out_scale = float(full_width) ** (-0.5)
    partial_value = lax.dot_general(
        all_calib, pruned_weight, (((1,), (1,)), ((), ())), preferred_element_type=jnp.float32
    )
    token_count = partial_value.shape[0]
    own_rows = lax.psum_scatter(
        (partial_value * out_scale).astype(jnp.bfloat16), "mp", scatter_dimension=0, tiled=True
    )
    per_col = row_parts // mp_parts
    pairs = []
    for r in range(row_parts):
        for m in range(mp_parts):
            target = ((r % per_col) * mp_parts + m) * mp_parts + r // per_col
            pairs.append((r * mp_parts + m, target))
    moved = lax.ppermute(own_rows, ("rows", "mp"), pairs)
    left = lax.all_gather(own_rows, "mp", axis=0, tiled=True)
    right = lax.all_gather(moved, "rows", axis=0, tiled=False)
    right = right.reshape(per_col, token_count, rows_dev)
    gram_block = gram_of(left, right, token_count)
    return (pruned_weight, gram_block)


def solution(mesh):
    return jax.shard_map(
        shards,
        mesh=mesh,
        in_specs=(P("rows", "mp"), P("rows", "mp"), P("rows", "mp"), P()),
        out_specs=(P("rows", "mp"), P("rows", "mp")),
        check_vma=False,
    )
```

```python
import functools

import jax
import jax.numpy as jnp
from jax import lax
from jax.experimental import pallas as pl
from jax.experimental.pallas import tpu as pltpu
from jax.sharding import PartitionSpec as P

BLOCK = 128
SUB = 8


def split3(value):
    first = value.astype(jnp.bfloat16)
    rest = value - first.astype(jnp.float32)
    second = rest.astype(jnp.bfloat16)
    third = (rest - second.astype(jnp.float32)).astype(jnp.bfloat16)
    return first, second, third


def sweep_block(tiles):
    lane = lax.broadcasted_iota(jnp.int32, (SUB, BLOCK), 1)
    sublane = lax.broadcasted_iota(jnp.int32, (SUB, BLOCK), 0)
    wide = (SUB, BLOCK)
    for p in range(0, BLOCK, 2):
        q = p + 1
        own, s = p // SUB, p % SUB
        row_p = jnp.broadcast_to(tiles[own][s : s + 1, :], wide)
        row_q = jnp.broadcast_to(tiles[own][s + 1 : s + 2, :], wide)
        d_p = jnp.broadcast_to(row_p[:, p : p + 1], wide)
        off = jnp.broadcast_to(row_p[:, q : q + 1], wide)
        d_q = jnp.broadcast_to(row_q[:, q : q + 1], wide)
        inv_p = 1.0 / d_p
        ratio = off * inv_p
        m_qq = 1.0 / (d_q - off * ratio)
        m_pq = -ratio * m_qq
        m_pp = inv_p - ratio * m_pq
        is_p, is_q = lane == p, lane == q
        u_p = m_pp * row_p + m_pq * row_q
        u_q = m_pq * row_p + m_qq * row_q
        u_p = jnp.where(is_p, -m_pp, jnp.where(is_q, -m_pq, u_p))
        u_q = jnp.where(is_p, -m_pq, jnp.where(is_q, -m_qq, u_q))
        pivot = is_p | is_q
        new = []
        for t in range(len(tiles)):
            col_p = jnp.broadcast_to(tiles[t][:, p : p + 1], wide)
            col_q = jnp.broadcast_to(tiles[t][:, q : q + 1], wide)
            value = jnp.where(pivot, 0.0, tiles[t]) - col_p * u_p - col_q * u_q
            if t == own:
                value = jnp.where(sublane == s, u_p, jnp.where(sublane == s + 1, u_q, value))
            new.append(value)
        tiles = new
    return tiles


def invert_kernel(low_ref, out_ref, neg_ref, rhs_ref, pivot_ref):
    count = out_ref.shape[0] // BLOCK
    at = 0
    for i in range(count):
        for j in range(i + 1):
            block = low_ref[:, at : at + BLOCK]
            at += BLOCK
            out_ref[i * BLOCK : (i + 1) * BLOCK, j * BLOCK : (j + 1) * BLOCK] = block
            if j < i:
                out_ref[j * BLOCK : (j + 1) * BLOCK, i * BLOCK : (i + 1) * BLOCK] = block.T

    def stage(k, carry):
        here = pl.ds(pl.multiple_of(k * BLOCK, BLOCK), BLOCK)
        diag = out_ref[here, here]
        tiles = [diag[t * SUB : (t + 1) * SUB, :] for t in range(BLOCK // SUB)]
        tiles = sweep_block(tiles)
        for t in range(BLOCK // SUB):
            neg_ref[t * SUB : (t + 1) * SUB, :] = tiles[t]
        neg = neg_ref[...]
        r1, r2, r3 = split3(out_ref[here, :])
        a1, a2, a3 = split3(-neg)
        pivot_ref[...] = jnp.dot(
            jnp.concatenate([a1, a1, a2, a2, a1, a3], axis=1),
            jnp.concatenate([r1, r2, r1, r2, r3, r1], axis=0),
            preferred_element_type=jnp.float32,
        )
        pivot_ref[:, here] = neg
        b1, b2, b3 = split3(pivot_ref[...])
        for slot, part in enumerate((b1, b2, b1, b2, b3, b1)):
            rhs_ref[slot * BLOCK : (slot + 1) * BLOCK, :] = part

        def update(i, inner):
            rows = pl.ds(pl.multiple_of(i * BLOCK, BLOCK), BLOCK)
            c1, c2, c3 = split3(out_ref[rows, here])
            out_ref[rows, here] = jnp.zeros((BLOCK, BLOCK), jnp.float32)
            out_ref[rows, :] -= jnp.dot(
                jnp.concatenate([c1, c1, c2, c2, c1, c3], axis=1),
                rhs_ref[...],
                preferred_element_type=jnp.float32,
            )
            return inner

        lax.fori_loop(0, count, update, 0)
        out_ref[here, :] = pivot_ref[...]
        return carry

    lax.fori_loop(0, count, stage, 0)


def minus_inverse(low, order):
    vmem = pl.BlockSpec(memory_space=pltpu.VMEM)
    return pl.pallas_call(
        invert_kernel,
        out_shape=jax.ShapeDtypeStruct((order, order), jnp.float32),
        in_specs=[vmem],
        out_specs=vmem,
        scratch_shapes=[
            pltpu.VMEM((BLOCK, BLOCK), jnp.float32),
            pltpu.VMEM((6 * BLOCK, order), jnp.bfloat16),
            pltpu.VMEM((BLOCK, order), jnp.float32),
        ],
        compiler_params=pltpu.CompilerParams(vmem_limit_bytes=32 * 1024 * 1024),
        cost_estimate=pl.CostEstimate(
            flops=60_000_000_000, bytes_accessed=2 * order * order * 4, transcendentals=0
        ),
    )(low)


def pick_columns_kernel(places_ref, factor_ref, columns_ref, low_ref):
    j = pl.program_id(0)
    columns_ref[...] = jnp.where(places_ref[1, j] != 0, factor_ref[...], 0.0)
    for i in range(places_ref.shape[1]):

        @pl.when(i >= j)
        def _():
            rows = pl.ds(pl.multiple_of(places_ref[2, i] * BLOCK, BLOCK), BLOCK)
            lanes = pl.ds(pl.multiple_of((i * (i + 1) // 2 + j) * BLOCK, BLOCK), BLOCK)
            low_ref[:, lanes] = jnp.where(places_ref[3, i] != 0, columns_ref[rows, :], 0.0)


def pick_columns(places, factor):
    count = places.shape[1]
    rows = factor.shape[0]
    lanes = count * (count + 1) // 2 * BLOCK
    return pl.pallas_call(
        pick_columns_kernel,
        out_shape=(
            jax.ShapeDtypeStruct((rows, count * BLOCK), jnp.float32),
            jax.ShapeDtypeStruct((BLOCK, lanes), jnp.float32),
        ),
        grid_spec=pltpu.PrefetchScalarGridSpec(
            num_scalar_prefetch=1,
            grid=(count,),
            in_specs=[pl.BlockSpec((rows, BLOCK), lambda j, places: (0, places[0, j]))],
            out_specs=(
                pl.BlockSpec((rows, BLOCK), lambda j, places: (0, j)),
                pl.BlockSpec((BLOCK, lanes), lambda j, places: (0, 0)),
            ),
        ),
    )(places, factor)


def pick_rows_kernel(places_ref, weight_ref, out_ref):
    inside = places_ref[3, pl.program_id(0)] != 0
    value = weight_ref[...].astype(jnp.float32)
    out_ref[...] = jnp.where(inside, value, 0.0).astype(jnp.bfloat16)


def pick_rows(places, weight):
    count = places.shape[1]
    width = weight.shape[1]
    return pl.pallas_call(
        pick_rows_kernel,
        out_shape=jax.ShapeDtypeStruct((count * BLOCK, width), jnp.bfloat16),
        grid_spec=pltpu.PrefetchScalarGridSpec(
            num_scalar_prefetch=1,
            grid=(count,),
            in_specs=[pl.BlockSpec((BLOCK, width), lambda i, places: (places[2, i], 0))],
            out_specs=pl.BlockSpec((BLOCK, width), lambda i, places: (i, 0)),
        ),
    )(places, weight)


def gram_kernel(token_count, left_ref, right_ref, out_ref):
    out_ref[...] = lax.dot_general(
        left_ref[...],
        right_ref[0],
        (((0,), (0,)), ((), ())),
        preferred_element_type=jnp.float32,
    ) / token_count


def gram_of(left, right, token_count):
    tokens, rows = left.shape
    parts, _, width = right.shape
    tile = min(rows, 256)
    return pl.pallas_call(
        functools.partial(gram_kernel, token_count),
        grid=(parts, rows // tile),
        in_specs=[
            pl.BlockSpec((tokens, tile), lambda c, i: (0, i)),
            pl.BlockSpec((1, tokens, width), lambda c, i: (c, 0, 0)),
        ],
        out_specs=pl.BlockSpec((tile, width), lambda c, i: (i, c)),
        out_shape=jax.ShapeDtypeStruct((rows, parts * width), jnp.float32),
    )(left, right)


def shards(calib, weight, inverse_factor, pruned_blocks):
    rows_dev = weight.shape[0]
    width_dev = weight.shape[1]
    row_parts = lax.axis_size("rows")
    mp_parts = lax.axis_size("mp")
    full_width = width_dev * mp_parts
    row_start = lax.axis_index("rows") * rows_dev
    col_start = lax.axis_index("mp") * width_dev
    starts = pruned_blocks * BLOCK
    block_count = pruned_blocks.shape[0]
    col_offsets = starts - col_start
    row_offsets = starts - row_start
    places = jnp.stack(
        [
            jnp.clip(col_offsets, 0, width_dev - BLOCK) // BLOCK,
            ((col_offsets >= 0) & (col_offsets < width_dev)).astype(jnp.int32),
            jnp.clip(row_offsets, 0, rows_dev - BLOCK) // BLOCK,
            ((row_offsets >= 0) & (row_offsets < rows_dev)).astype(jnp.int32),
        ]
    ).astype(jnp.int32)
    columns, own_low = pick_columns(places, inverse_factor)
    own_kept = pick_rows(places, weight)
    share = lax.psum_scatter(own_low, "mp", scatter_dimension=0, tiled=True)
    share = lax.psum(share, "rows")
    share, own_kept, calib, columns = lax.optimization_barrier((share, own_kept, calib, columns))
    low = lax.all_gather(share, "mp", axis=0, tiled=True)
    kept_rows = lax.psum(own_kept, "rows")
    own_columns = lax.psum_scatter(columns, "mp", scatter_dimension=0, tiled=True)
    all_calib = lax.all_gather(calib, "rows", axis=0, tiled=True)

    negative = minus_inverse(low, block_count * BLOCK)
    negative, all_calib, own_columns = lax.optimization_barrier((negative, all_calib, own_columns))
    own_factors = -lax.dot_general(
        own_columns,
        negative,
        (((1,), (0,)), ((), ())),
        precision=lax.Precision.HIGHEST,
        preferred_element_type=jnp.float32,
    )
    factors = lax.all_gather(own_factors.astype(jnp.bfloat16), "mp", axis=0, tiled=True)
    update = lax.dot_general(
        factors, kept_rows, (((1,), (0,)), ((), ())), preferred_element_type=jnp.float32
    )
    block_ids = (row_start + jnp.arange(rows_dev, dtype=jnp.int32)) // BLOCK
    pruned = jnp.any(block_ids[:, None] == pruned_blocks[None, :], axis=1)
    pruned_weight = jnp.where(
        pruned[:, None], 0.0, weight.astype(jnp.float32) - update
    ).astype(jnp.bfloat16)
    out_scale = float(full_width) ** (-0.5)
    partial_value = lax.dot_general(
        all_calib, pruned_weight, (((1,), (1,)), ((), ())), preferred_element_type=jnp.float32
    )
    token_count = partial_value.shape[0]
    own_rows = lax.psum_scatter(
        (partial_value * out_scale).astype(jnp.bfloat16), "mp", scatter_dimension=0, tiled=True
    )
    per_col = row_parts // mp_parts
    pairs = []
    for r in range(row_parts):
        for m in range(mp_parts):
            target = ((r % per_col) * mp_parts + m) * mp_parts + r // per_col
            pairs.append((r * mp_parts + m, target))
    moved = lax.ppermute(own_rows, ("rows", "mp"), pairs)
    own_rows, moved = lax.optimization_barrier((own_rows, moved))
    left = lax.all_gather(own_rows, "mp", axis=0, tiled=True)
    right = lax.all_gather(moved, "rows", axis=0, tiled=False)
    right = right.reshape(per_col, token_count, rows_dev)
    gram_block = gram_of(left, right, token_count)
    return (pruned_weight, gram_block)


def solution(mesh):
    return jax.shard_map(
        shards,
        mesh=mesh,
        in_specs=(P("rows", "mp"), P("rows", "mp"), P("rows", "mp"), P()),
        out_specs=(P("rows", "mp"), P("rows", "mp")),
        check_vma=False,
    )
```

```python
import functools

import jax
import jax.numpy as jnp
from jax import lax
from jax.experimental import pallas as pl
from jax.experimental.pallas import tpu as pltpu
from jax.sharding import PartitionSpec as P

BLOCK = 128
SUB = 8
GROUP = 4


def split3(value):
    first = value.astype(jnp.bfloat16)
    rest = value - first.astype(jnp.float32)
    second = rest.astype(jnp.bfloat16)
    third = (rest - second.astype(jnp.float32)).astype(jnp.bfloat16)
    return first, second, third


def sweep_block(tiles):
    lane = lax.broadcasted_iota(jnp.int32, (SUB, BLOCK), 1)
    sublane = lax.broadcasted_iota(jnp.int32, (SUB, BLOCK), 0)
    wide = (SUB, BLOCK)
    for p in range(0, BLOCK, GROUP):
        own, s = p // SUB, p % SUB
        rows = [
            jnp.broadcast_to(tiles[own][s + a : s + a + 1, :], wide) for a in range(GROUP)
        ]
        small = {}
        for a in range(GROUP):
            for b in range(a, GROUP):
                small[a, b] = jnp.broadcast_to(rows[a][:, p + b : p + b + 1], wide)
        for k in range(GROUP):
            inv = 1.0 / small[k, k]
            old = {a: small[min(a, k), max(a, k)] for a in range(GROUP) if a != k}
            scaled = {a: value * inv for a, value in old.items()}
            for a in old:
                for b in old:
                    if a <= b:
                        small[a, b] = small[a, b] - old[a] * scaled[b]
                small[min(a, k), max(a, k)] = scaled[a]
            small[k, k] = -inv
        pivots = [lane == p + a for a in range(GROUP)]
        updates = []
        for a in range(GROUP):
            update = -small[0, a] * rows[0]
            for b in range(1, GROUP):
                update = update - small[min(a, b), max(a, b)] * rows[b]
            for b in range(GROUP):
                update = jnp.where(pivots[b], small[min(a, b), max(a, b)], update)
            updates.append(update)
        inside = (lane >= p) & (lane < p + GROUP)
        new = []
        for t in range(len(tiles)):
            value = jnp.where(inside, 0.0, tiles[t])
            for a in range(GROUP):
                column = jnp.broadcast_to(tiles[t][:, p + a : p + a + 1], wide)
                value = value - column * updates[a]
            if t == own:
                for a in range(GROUP):
                    value = jnp.where(sublane == s + a, updates[a], value)
            new.append(value)
        tiles = new
    return tiles


def invert_kernel(low_ref, out_ref, neg_ref, rhs_ref, pivot_ref):
    count = out_ref.shape[0] // BLOCK
    at = 0
    for i in range(count):
        for j in range(i + 1):
            block = low_ref[:, at : at + BLOCK]
            at += BLOCK
            out_ref[i * BLOCK : (i + 1) * BLOCK, j * BLOCK : (j + 1) * BLOCK] = block
            if j < i:
                out_ref[j * BLOCK : (j + 1) * BLOCK, i * BLOCK : (i + 1) * BLOCK] = block.T

    def stage(k, carry):
        here = pl.ds(pl.multiple_of(k * BLOCK, BLOCK), BLOCK)
        diag = out_ref[here, here]
        tiles = [diag[t * SUB : (t + 1) * SUB, :] for t in range(BLOCK // SUB)]
        tiles = sweep_block(tiles)
        for t in range(BLOCK // SUB):
            neg_ref[t * SUB : (t + 1) * SUB, :] = tiles[t]
        neg = neg_ref[...]
        r1, r2, r3 = split3(out_ref[here, :])
        a1, a2, a3 = split3(-neg)
        pivot_ref[...] = jnp.dot(
            jnp.concatenate([a1, a1, a2, a2, a1, a3], axis=1),
            jnp.concatenate([r1, r2, r1, r2, r3, r1], axis=0),
            preferred_element_type=jnp.float32,
        )
        pivot_ref[:, here] = neg
        b1, b2, b3 = split3(pivot_ref[...])
        for slot, part in enumerate((b1, b2, b1, b2, b3, b1)):
            rhs_ref[slot * BLOCK : (slot + 1) * BLOCK, :] = part

        def update(i, inner):
            rows = pl.ds(pl.multiple_of(i * BLOCK, BLOCK), BLOCK)
            c1, c2, c3 = split3(out_ref[rows, here])
            out_ref[rows, here] = jnp.zeros((BLOCK, BLOCK), jnp.float32)
            out_ref[rows, :] -= jnp.dot(
                jnp.concatenate([c1, c1, c2, c2, c1, c3], axis=1),
                rhs_ref[...],
                preferred_element_type=jnp.float32,
            )
            return inner

        lax.fori_loop(0, count, update, 0)
        out_ref[here, :] = pivot_ref[...]
        return carry

    lax.fori_loop(0, count, stage, 0)


def minus_inverse(low, order):
    vmem = pl.BlockSpec(memory_space=pltpu.VMEM)
    return pl.pallas_call(
        invert_kernel,
        out_shape=jax.ShapeDtypeStruct((order, order), jnp.float32),
        in_specs=[vmem],
        out_specs=vmem,
        scratch_shapes=[
            pltpu.VMEM((BLOCK, BLOCK), jnp.float32),
            pltpu.VMEM((6 * BLOCK, order), jnp.bfloat16),
            pltpu.VMEM((BLOCK, order), jnp.float32),
        ],
        compiler_params=pltpu.CompilerParams(vmem_limit_bytes=32 * 1024 * 1024),
        cost_estimate=pl.CostEstimate(
            flops=60_000_000_000, bytes_accessed=2 * order * order * 4, transcendentals=0
        ),
    )(low)


def pick_columns_kernel(places_ref, factor_ref, columns_ref, low_ref):
    j = pl.program_id(0)
    columns_ref[...] = jnp.where(places_ref[1, j] != 0, factor_ref[...], 0.0)
    for i in range(places_ref.shape[1]):

        @pl.when(i >= j)
        def _():
            rows = pl.ds(pl.multiple_of(places_ref[2, i] * BLOCK, BLOCK), BLOCK)
            lanes = pl.ds(pl.multiple_of((i * (i + 1) // 2 + j) * BLOCK, BLOCK), BLOCK)
            low_ref[:, lanes] = jnp.where(places_ref[3, i] != 0, columns_ref[rows, :], 0.0)


def pick_columns(places, factor):
    count = places.shape[1]
    rows = factor.shape[0]
    lanes = count * (count + 1) // 2 * BLOCK
    return pl.pallas_call(
        pick_columns_kernel,
        out_shape=(
            jax.ShapeDtypeStruct((rows, count * BLOCK), jnp.float32),
            jax.ShapeDtypeStruct((BLOCK, lanes), jnp.float32),
        ),
        grid_spec=pltpu.PrefetchScalarGridSpec(
            num_scalar_prefetch=1,
            grid=(count,),
            in_specs=[pl.BlockSpec((rows, BLOCK), lambda j, places: (0, places[0, j]))],
            out_specs=(
                pl.BlockSpec((rows, BLOCK), lambda j, places: (0, j)),
                pl.BlockSpec((BLOCK, lanes), lambda j, places: (0, 0)),
            ),
        ),
    )(places, factor)


def pick_rows_kernel(places_ref, weight_ref, out_ref):
    inside = places_ref[3, pl.program_id(0)] != 0
    value = weight_ref[...].astype(jnp.float32)
    out_ref[...] = jnp.where(inside, value, 0.0).astype(jnp.bfloat16)


def pick_rows(places, weight):
    count = places.shape[1]
    width = weight.shape[1]
    return pl.pallas_call(
        pick_rows_kernel,
        out_shape=jax.ShapeDtypeStruct((count * BLOCK, width), jnp.bfloat16),
        grid_spec=pltpu.PrefetchScalarGridSpec(
            num_scalar_prefetch=1,
            grid=(count,),
            in_specs=[pl.BlockSpec((BLOCK, width), lambda i, places: (places[2, i], 0))],
            out_specs=pl.BlockSpec((BLOCK, width), lambda i, places: (i, 0)),
        ),
    )(places, weight)


def gram_kernel(token_count, left_ref, right_ref, out_ref):
    out_ref[...] = lax.dot_general(
        left_ref[...],
        right_ref[0],
        (((0,), (0,)), ((), ())),
        preferred_element_type=jnp.float32,
    ) / token_count


def gram_of(left, right, token_count):
    tokens, rows = left.shape
    parts, _, width = right.shape
    tile = min(rows, 256)
    return pl.pallas_call(
        functools.partial(gram_kernel, token_count),
        grid=(parts, rows // tile),
        in_specs=[
            pl.BlockSpec((tokens, tile), lambda c, i: (0, i)),
            pl.BlockSpec((1, tokens, width), lambda c, i: (c, 0, 0)),
        ],
        out_specs=pl.BlockSpec((tile, width), lambda c, i: (i, c)),
        out_shape=jax.ShapeDtypeStruct((rows, parts * width), jnp.float32),
    )(left, right)


def shards(calib, weight, inverse_factor, pruned_blocks):
    rows_dev = weight.shape[0]
    width_dev = weight.shape[1]
    row_parts = lax.axis_size("rows")
    mp_parts = lax.axis_size("mp")
    full_width = width_dev * mp_parts
    row_start = lax.axis_index("rows") * rows_dev
    col_start = lax.axis_index("mp") * width_dev
    starts = pruned_blocks * BLOCK
    block_count = pruned_blocks.shape[0]
    col_offsets = starts - col_start
    row_offsets = starts - row_start
    places = jnp.stack(
        [
            jnp.clip(col_offsets, 0, width_dev - BLOCK) // BLOCK,
            ((col_offsets >= 0) & (col_offsets < width_dev)).astype(jnp.int32),
            jnp.clip(row_offsets, 0, rows_dev - BLOCK) // BLOCK,
            ((row_offsets >= 0) & (row_offsets < rows_dev)).astype(jnp.int32),
        ]
    ).astype(jnp.int32)
    columns, own_low = pick_columns(places, inverse_factor)
    low = lax.psum(own_low, ("rows", "mp"))
    own_columns = lax.psum_scatter(columns, "mp", scatter_dimension=0, tiled=True)
    all_calib = lax.all_gather(calib, "rows", axis=0, tiled=True)
    low, own_kept = lax.optimization_barrier((low, pick_rows(places, weight)))
    kept_rows = lax.psum(own_kept, "rows")

    negative = minus_inverse(low, block_count * BLOCK)
    negative, all_calib, own_columns = lax.optimization_barrier((negative, all_calib, own_columns))
    own_factors = -lax.dot_general(
        own_columns,
        negative,
        (((1,), (0,)), ((), ())),
        precision=lax.Precision.HIGHEST,
        preferred_element_type=jnp.float32,
    )
    factors = lax.all_gather(own_factors.astype(jnp.bfloat16), "mp", axis=0, tiled=True)
    update = lax.dot_general(
        factors, kept_rows, (((1,), (0,)), ((), ())), preferred_element_type=jnp.float32
    )
    block_ids = (row_start + jnp.arange(rows_dev, dtype=jnp.int32)) // BLOCK
    pruned = jnp.any(block_ids[:, None] == pruned_blocks[None, :], axis=1)
    pruned_weight = jnp.where(
        pruned[:, None], 0.0, weight.astype(jnp.float32) - update
    ).astype(jnp.bfloat16)
    out_scale = float(full_width) ** (-0.5)
    partial_value = lax.dot_general(
        all_calib, pruned_weight, (((1,), (1,)), ((), ())), preferred_element_type=jnp.float32
    )
    token_count = partial_value.shape[0]
    own_rows = lax.psum_scatter(
        (partial_value * out_scale).astype(jnp.bfloat16), "mp", scatter_dimension=0, tiled=True
    )
    per_col = row_parts // mp_parts
    pairs = []
    for r in range(row_parts):
        for m in range(mp_parts):
            target = ((r % per_col) * mp_parts + m) * mp_parts + r // per_col
            pairs.append((r * mp_parts + m, target))
    moved = lax.ppermute(own_rows, ("rows", "mp"), pairs)
    left = lax.all_gather(own_rows, "mp", axis=0, tiled=True)
    right = lax.all_gather(moved, "rows", axis=0, tiled=False)
    right = right.reshape(per_col, token_count, rows_dev)
    gram_block = gram_of(left, right, token_count)
    return (pruned_weight, gram_block)


def solution(mesh):
    return jax.shard_map(
        shards,
        mesh=mesh,
        in_specs=(P("rows", "mp"), P("rows", "mp"), P("rows", "mp"), P()),
        out_specs=(P("rows", "mp"), P("rows", "mp")),
        check_vma=False,
    )
```
